32 devices in a mesh: ctx: 8 (over z, x), exp: 4 (over y, core).
Axes of the slice: x: 2, y: 2, z: 4, core: 2. Of those that a mesh axis runs over, the one named last changes fastest.
Arguments:
- hidden_states: bfloat16 [4096, 4096], P(('ctx', 'exp')), may hold values from -70 to 70
- upstream: bfloat16 [4096, 4096], P(('ctx', 'exp')), may hold values from -6 to 6
- norm_gain: float32 [4096], replicated, may hold values from 0.5 to 1.5
- router: bfloat16 [4096, 8], replicated, may hold values from -4 to 4
- expert_ids: int32 [4096, 8], P(('ctx', 'exp')), may hold values from 0 to 7, as said below
- w_gate: bfloat16 [8, 4096, 1536], P('ctx', None, 'exp'), may hold values from -0.09375 to 0.09375
- w_up: bfloat16 [8, 4096, 1536], P('ctx', None, 'exp'), may hold values from -0.09375 to 0.09375
- w_down: bfloat16 [8, 1536, 4096], P('ctx', 'exp'), may hold values from -0.15625 to 0.15625
Outputs:
- grad_input: bfloat16 [4096, 4096], P(('ctx', 'exp'))
The draws below stay inside these ranges and needn't reach their ends.
Inputs may be any that keep to these rules, and one draw needn't show every extreme that they name: `expert_ids`: A token's 8 entries differ. Among the rows of one device, no expert is named in column 0 by more than 24 rows, and in every device's rows one expert is named there by exactly 24.
All inputs are finite; a program needn't handle non-finite values.
Results may differ from the reference program's by a relative error of at most 0.012.
Values may be sent and summed in bfloat16 or wider, within the bound.
A program may use at most 128 MiB of HBM per device.

```python
import jax
import jax.numpy as jnp
from jax import lax

D = 4096
FF = 1536
TOPK = 8
TOK_DEV = 128
E = 8
TOKENS = 4096
CAP = 24
N_CTX = 8
N_EXP = 4


def draw_hidden_states(key, part):
    key_base, key_rows, key_cols = jax.random.split(key, 3)
    row_scale = jnp.exp(jax.random.uniform(key_rows, (TOKENS, 1), jnp.float32, 0.0, 0.693147))
    col_scale = jnp.exp(jax.random.uniform(key_cols, (1, D), jnp.float32, 0.0, 2.302585))
    base_values = jnp.clip(jax.random.normal(key_base, (TOKENS, D), jnp.float32), -3.5, 3.5)
    return (base_values * row_scale * col_scale).astype(jnp.bfloat16)


def draw_router(key, part):
    key_base, key_scale = jax.random.split(key, 2)
    weights = jnp.clip(jax.random.normal(key_base, (D, E), jnp.float32), -4.0, 4.0)
    scales = jnp.exp(jax.random.uniform(key_scale, (1, E), jnp.float32, -1.049822, -0.356675))
    values = weights * scales
    return jnp.clip(values * D ** (-0.5), -4.0, 4.0).astype(jnp.bfloat16)


def one_block(block_key):
    key_full, key_score, key_shuffle, key_other = jax.random.split(block_key, 4)
    slot_total = E * CAP
    slot_ids = jnp.arange(slot_total, dtype=jnp.int32)
    owner_expert = slot_ids // CAP
    full_expert = jax.random.randint(key_full, (), 0, E, dtype=jnp.int32)
    random_score = jax.random.randint(key_score, (slot_total,), 0, 1 << 19, dtype=jnp.int32)
    scores = jnp.where(owner_expert == full_expert, slot_ids - slot_total, random_score * slot_total + slot_ids)
    ranking = jnp.argsort(scores)
    picked = owner_expert[ranking[:TOK_DEV]]
    shuffle_score = jax.random.randint(key_shuffle, (TOK_DEV,), 0, 1 << 19, dtype=jnp.int32) * TOK_DEV + jnp.arange(TOK_DEV, dtype=jnp.int32)
    picked = picked[jnp.argsort(shuffle_score)]
    labels = jnp.arange(E, dtype=jnp.int32)
    other_score = jax.random.randint(key_other, (TOK_DEV, E), 0, 1 << 19, dtype=jnp.int32) * E + labels[None, :]
    other_score = jnp.where(labels[None, :] == picked[:, None], -1, other_score)
    ranked = jnp.argsort(other_score, axis=1)[:, :TOPK]
    return ranked.astype(jnp.int32)


def draw_expert_ids(key, part):
    block_keys = jax.random.split(key, TOKENS // TOK_DEV)
    return jax.vmap(one_block)(block_keys).reshape(TOKENS, TOPK)


def shard_levels(rng, extent, shards, low, high):
    def one(dim, parts):
        steps = jax.random.uniform(jax.random.fold_in(jax.random.fold_in(rng, 6), dim), (parts,), jnp.float32, low / len(shards), high / len(shards))
        return jnp.repeat(jnp.exp(steps), extent[dim] // parts).reshape((-1,) + (1,) * (len(extent) - dim - 1))

    factor_of = one(*shards[0])
    for cut in shards[1:]:
        factor_of = factor_of * one(*cut)
    return factor_of


def gaussian(own_key, shape, scale, limit, shards=(), kind=jnp.bfloat16):
    gain = shard_levels(own_key, shape, shards, -0.22, 0.18) if shards else 1.0
    entries = jax.random.normal(own_key, shape, jnp.float32) * scale * gain
    return jnp.minimum(jnp.maximum(entries, -limit), limit).astype(kind)


def setup_inputs(seed: int = 0) -> dict:
    arg_keys = jax.random.split(jax.random.key(seed), 9)
    return {
        "hidden_states": draw_hidden_states(jax.random.fold_in(arg_keys[8], 71), 0),
        "upstream": gaussian(arg_keys[1], (TOKENS, D), 1.0, 6.0, ((0, 32),)),
        "norm_gain": jnp.clip(1.0 + 0.1 * jax.random.normal(arg_keys[2], (D,), jnp.float32), 0.5, 1.5),
        "router": draw_router(jax.random.fold_in(arg_keys[8], 71), 0),
        "expert_ids": draw_expert_ids(jax.random.fold_in(arg_keys[8], 71), 0),
        "w_gate": gaussian(arg_keys[5], (E, D, FF), D ** -0.5, 0.09375, ((0, 8), (2, 4))),
        "w_up": gaussian(arg_keys[6], (E, D, FF), D ** -0.5, 0.09375, ((0, 8), (2, 4))),
        "w_down": gaussian(arg_keys[7], (E, FF, D), FF ** -0.5, 0.15625, ((0, 8), (1, 4))),
    }


EPSILON = 1e-06

def silu_parts(pre_value):
    sigmoid_value = jax.nn.sigmoid(pre_value)
    return (pre_value * sigmoid_value, sigmoid_value * (1.0 + pre_value * (1.0 - sigmoid_value)))

def reference(hidden_states, upstream, norm_gain, router, expert_ids, w_gate, w_up, w_down):
    widened = hidden_states.astype(jnp.float32)
    inverse = lax.rsqrt(lax.optimization_barrier(jnp.mean(widened * widened, axis=1, keepdims=True)) + EPSILON)
    normed = (widened * inverse * norm_gain).astype(jnp.bfloat16)
    logits = jnp.dot(normed, router, preferred_element_type=jnp.float32)
    probability = jax.nn.softmax(logits, axis=1)
    labels = jnp.arange(E, dtype=jnp.int32)
    chosen = (expert_ids[:, :, None] == labels).astype(jnp.float32)
    primary = chosen[:, 0, :]
    member = lax.optimization_barrier(jnp.sum(chosen, axis=1))
    top_prob = lax.optimization_barrier(jnp.sum(probability * primary, axis=1))
    route_mass = lax.optimization_barrier(jnp.sum(probability * member, axis=1))
    gate_value = top_prob / route_mass
    scaled_grad = (gate_value[:, None] * upstream.astype(jnp.float32)).astype(jnp.bfloat16)
    blocks = primary.reshape(N_CTX * N_EXP, TOK_DEV, E)
    before = jnp.cumsum(blocks, axis=1) - blocks
    slot_index = lax.optimization_barrier(jnp.sum(before * blocks, axis=2)).reshape(TOKENS).astype(jnp.int32)
    position = jnp.arange(TOKENS, dtype=jnp.int32)
    block_id = position // TOK_DEV
    row_index = block_id % N_EXP * (N_CTX * CAP) + block_id // N_EXP * CAP + slot_index
    token_of = jnp.full((E, N_EXP * N_CTX * CAP), TOKENS, jnp.int32).at[expert_ids[:, 0], row_index].set(position)
    shard_width = FF // N_EXP
    pad_row = jnp.zeros((1, D), jnp.bfloat16)
    normed_pad = jnp.concatenate([normed, pad_row], axis=0)
    grad_pad = jnp.concatenate([scaled_grad, pad_row], axis=0)

    def per_expert(totals, member_array):
        out_tokens, back_tokens = totals
        gate_block, up_block, down_block, token_rows = member_array
        expert_rows = normed_pad[token_rows]
        grad_rows = grad_pad[token_rows]
        row_count = expert_rows.shape[0]
        pre_gate = jnp.dot(expert_rows, gate_block, preferred_element_type=jnp.float32)
        pre_up = jnp.dot(expert_rows, up_block, preferred_element_type=jnp.float32)
        activated, act_slope = silu_parts(pre_gate)
        hidden = (activated * pre_up).astype(jnp.bfloat16)
        partials = jnp.einsum('rsf,sfd->srd', hidden.reshape(row_count, N_EXP, shard_width).astype(jnp.float32), down_block.reshape(N_EXP, shard_width, D).astype(jnp.float32))
        partials = lax.optimization_barrier(partials.astype(jnp.bfloat16)).astype(jnp.float32)
        expert_out = lax.optimization_barrier(jnp.sum(partials, axis=0)).astype(jnp.bfloat16)
        hidden_grad = lax.dot_general(grad_rows, down_block, (((1,), (1,)), ((), ())), preferred_element_type=jnp.float32)
        grad_pre_gate = (hidden_grad * pre_up * act_slope).astype(jnp.bfloat16)
        grad_pre_up = (hidden_grad * activated).astype(jnp.bfloat16)
        grad_partials = jnp.einsum('rsf,dsf->srd', grad_pre_gate.reshape(row_count, N_EXP, shard_width).astype(jnp.float32), gate_block.reshape(D, N_EXP, shard_width).astype(jnp.float32))
        grad_partials = grad_partials + jnp.einsum('rsf,dsf->srd', grad_pre_up.reshape(row_count, N_EXP, shard_width).astype(jnp.float32), up_block.reshape(D, N_EXP, shard_width).astype(jnp.float32))
        grad_partials = lax.optimization_barrier(grad_partials.astype(jnp.bfloat16)).astype(jnp.float32)
        expert_grad = lax.optimization_barrier(jnp.sum(grad_partials, axis=0)).astype(jnp.bfloat16)
        return ((out_tokens.at[token_rows].set(expert_out), back_tokens.at[token_rows].set(expert_grad)), None)
    start_value = jnp.zeros((TOKENS + 1, D), jnp.bfloat16)
    finals, unused = lax.scan(per_expert, (start_value, start_value), (w_gate, w_up, w_down, token_of))
    expert_out = finals[0][:TOKENS].astype(jnp.float32)
    expert_grad = finals[1][:TOKENS].astype(jnp.float32)
    gate_grad = lax.optimization_barrier(jnp.sum(upstream.astype(jnp.float32) * expert_out, axis=1))
    prob_grad = gate_grad[:, None] * (primary / route_mass[:, None] - (top_prob / (route_mass * route_mass))[:, None] * member)
    logit_grad = probability * (prob_grad - lax.optimization_barrier(jnp.sum(probability * prob_grad, axis=1, keepdims=True)))
    normed_grad = expert_grad + jnp.dot(logit_grad, router.astype(jnp.float32).T, precision=lax.Precision.HIGHEST)
    scaled = normed_grad * norm_gain
    grad_input = inverse * scaled - widened * inverse ** 3 * lax.optimization_barrier(jnp.sum(scaled * widened, axis=1, keepdims=True)) / D
    return grad_input.astype(jnp.bfloat16)
```

```python
import jax
import jax.numpy as jnp
from jax import lax
from jax.sharding import PartitionSpec as P

EPSILON = 1e-06
F32 = jnp.float32
BF16 = jnp.bfloat16


def pick(rows_of, total, values):
    hot = (rows_of[None, :] == jnp.arange(total, dtype=jnp.int32)[:, None]).astype(BF16)
    return jnp.dot(hot, values, preferred_element_type=F32).astype(BF16)


def expert_math(normed_rows, up_rows, gate_block, up_block, down_block):
    pre_gate = jnp.dot(normed_rows, gate_block, preferred_element_type=F32)
    pre_up = jnp.dot(normed_rows, up_block, preferred_element_type=F32)
    raw_grad = lax.dot_general(
        up_rows, down_block, (((1,), (1,)), ((), ())), preferred_element_type=F32
    )
    sig = jax.nn.sigmoid(pre_gate)
    act = pre_gate * sig
    slope = sig * (1.0 + pre_gate * (1.0 - sig))
    hidden = (act * pre_up).astype(BF16).astype(F32)
    dots = jnp.sum(hidden * raw_grad, axis=1)
    grad_gate = (raw_grad * pre_up * slope).astype(BF16)
    grad_up = (raw_grad * act).astype(BF16)
    back = lax.dot_general(
        grad_gate, gate_block, (((1,), (1,)), ((), ())), preferred_element_type=F32
    ) + lax.dot_general(grad_up, up_block, (((1,), (1,)), ((), ())), preferred_element_type=F32)
    return back, dots


def exchange_collective(slots_normed, slots_up, gate_block, up_block, down_block):
    experts, capacity, width = slots_normed.shape

    def dispatch(shaped):
        moved = lax.all_to_all(shaped, "ctx", split_axis=0, concat_axis=0, tiled=True)
        return lax.all_gather(
            moved.reshape(experts * capacity, width), "exp", axis=0, tiled=True
        )

    back, dots = expert_math(
        dispatch(slots_normed), dispatch(slots_up), gate_block, up_block, down_block
    )
    summed = lax.psum_scatter(back.astype(BF16), "exp", scatter_dimension=0, tiled=True)
    dot_sum = lax.psum_scatter(dots, "exp", scatter_dimension=0, tiled=True)
    returned = lax.all_to_all(
        summed.reshape(experts, capacity, width), "ctx", split_axis=0, concat_axis=0, tiled=True
    )
    dot_back = lax.all_to_all(
        dot_sum.reshape(experts, capacity), "ctx", split_axis=0, concat_axis=0, tiled=True
    )
    return returned.reshape(experts * capacity, width), dot_back.reshape(experts * capacity)


def per_device(hidden_states, upstream, norm_gain, router, expert_ids, w_gate, w_up, w_down):
    tok_rows, model_width = hidden_states.shape
    experts = router.shape[1]
    capacity = 3 * tok_rows // (2 * experts)
    slot_total = experts * capacity
    labels = jnp.arange(experts, dtype=jnp.int32)
    chosen = (expert_ids[:, :, None] == labels).astype(F32)
    primary = chosen[:, 0, :]
    member = jnp.sum(chosen, axis=1)
    lower = (
        jnp.arange(tok_rows)[:, None] > jnp.arange(tok_rows)[None, :]
    ).astype(BF16)
    before = jnp.dot(lower, primary.astype(BF16), preferred_element_type=F32)
    slot_index = jnp.sum(before * primary, axis=1).astype(jnp.int32)
    target = expert_ids[:, 0] * capacity + slot_index

    widened = hidden_states.astype(F32)
    inverse = lax.rsqrt(jnp.mean(widened * widened, axis=1, keepdims=True) + EPSILON)
    normed = (widened * inverse * norm_gain).astype(BF16)

    slots_up = pick(target, slot_total, upstream).reshape(experts, capacity, model_width)
    slots_normed = pick(target, slot_total, normed).reshape(experts, capacity, model_width)
    returned, dots = exchange_collective(slots_normed, slots_up, w_gate[0], w_up[0], w_down[0])

    logits = jnp.dot(normed, router, preferred_element_type=F32)
    probability = jax.nn.softmax(logits, axis=1)
    top_prob = jnp.sum(probability * primary, axis=1)
    route_mass = jnp.sum(probability * member, axis=1)
    gate_value = top_prob / route_mass

    own = target[:, None] == jnp.arange(slot_total, dtype=jnp.int32)[None, :]
    raw_back = jnp.dot(own.astype(BF16), returned, preferred_element_type=F32)
    gate_grad = jnp.sum(jnp.where(own, dots[None, :], 0.0), axis=1)
    expert_grad = gate_value[:, None] * raw_back
    prob_grad = gate_grad[:, None] * (
        primary / route_mass[:, None] - (top_prob / (route_mass * route_mass))[:, None] * member
    )
    logit_grad = probability * (prob_grad - jnp.sum(probability * prob_grad, axis=1, keepdims=True))
    normed_grad = expert_grad + jnp.dot(
        logit_grad, router.astype(F32).T, precision=lax.Precision.HIGHEST
    )
    scaled = normed_grad * norm_gain
    grad_input = (
        inverse * scaled
        - widened * inverse**3 * jnp.sum(scaled * widened, axis=1, keepdims=True) / model_width
    )
    return grad_input.astype(BF16)


def solution(mesh):
    placed = (
        P(("ctx", "exp"), None),
        P(("ctx", "exp"), None),
        P(),
        P(),
        P(("ctx", "exp"), None),
        P("ctx", None, "exp"),
        P("ctx", None, "exp"),
        P("ctx", "exp", None),
    )
    return jax.shard_map(
        per_device, mesh=mesh, in_specs=placed, out_specs=P(("ctx", "exp"), None), check_vma=False
    )
```

```python
import functools

import jax
import jax.numpy as jnp
from jax import lax
from jax.experimental import pallas as pl
from jax.experimental.pallas import tpu as pltpu
from jax.sharding import PartitionSpec as P

EPSILON = 1e-06
F32 = jnp.float32
BF16 = jnp.bfloat16
LANES = 128
DEEP = 1024
WIDE = 512


def pick(rows_of, total, values):
    hot = (rows_of[None, :] == jnp.arange(total, dtype=jnp.int32)[:, None]).astype(BF16)
    return jnp.dot(hot, values, preferred_element_type=F32).astype(BF16)


def expert_math(normed_rows, up_rows, gate_block, up_block, down_block):
    pre_gate = jnp.dot(normed_rows, gate_block, preferred_element_type=F32)
    pre_up = jnp.dot(normed_rows, up_block, preferred_element_type=F32)
    raw_grad = lax.dot_general(
        up_rows, down_block, (((1,), (1,)), ((), ())), preferred_element_type=F32
    )
    sig = jax.nn.sigmoid(pre_gate)
    act = pre_gate * sig
    slope = sig * (1.0 + pre_gate * (1.0 - sig))
    hidden = (act * pre_up).astype(BF16).astype(F32)
    dots = jnp.sum(hidden * raw_grad, axis=1)
    grad_gate = (raw_grad * pre_up * slope).astype(BF16)
    grad_up = (raw_grad * act).astype(BF16)
    back = lax.dot_general(
        grad_gate, gate_block, (((1,), (1,)), ((), ())), preferred_element_type=F32
    ) + lax.dot_general(grad_up, up_block, (((1,), (1,)), ((), ())), preferred_element_type=F32)
    return back, dots


def exchange_collective(slots_normed, slots_up, gate_block, up_block, down_block):
    experts, capacity, width = slots_normed.shape

    def dispatch(shaped):
        moved = lax.all_to_all(shaped, "ctx", split_axis=0, concat_axis=0, tiled=True)
        return lax.all_gather(
            moved.reshape(experts * capacity, width), "exp", axis=0, tiled=True
        )

    back, dots = expert_math(
        dispatch(slots_normed), dispatch(slots_up), gate_block, up_block, down_block
    )
    summed = lax.psum_scatter(back.astype(BF16), "exp", scatter_dimension=0, tiled=True)
    dot_sum = lax.psum_scatter(dots, "exp", scatter_dimension=0, tiled=True)
    returned = lax.all_to_all(
        summed.reshape(experts, capacity, width), "ctx", split_axis=0, concat_axis=0, tiled=True
    )
    dot_back = lax.all_to_all(
        dot_sum.reshape(experts, capacity), "ctx", split_axis=0, concat_axis=0, tiled=True
    )
    return returned.reshape(experts * capacity, width), dot_back.reshape(experts * capacity)


def exclusive_or(left, right, count):
    total, bit = 0, 1
    while bit < count:
        total = total + bit * lax.rem(lax.div(left, bit) + lax.div(right, bit), 2)
        bit *= 2
    return total


def ordered(step, count):
    return lax.rem(step, 2) * (count // 2) + lax.div(step, 2)


def carry(total, width, capacity):
    dots = total[:capacity, width:] + total[capacity:, width:]
    high = dots.astype(BF16).astype(F32)
    return total[:, :width].astype(BF16), jnp.concatenate([high, dots - high], axis=0).astype(BF16)


def exchange_body(
    count, capacity, send_ref, gate_hbm, up_hbm, down_hbm, out_ref,
    both, down, rows, part, mate_in, mid, cross_in, done, acc_both, acc_down, grads,
    weight_sem, local_sem, send_sem, recv_sem,
):
    width = send_ref.shape[2]
    half = width // 2
    units = down.shape[0]
    tall = -(-capacity // 16) * 16
    skip = tall - capacity
    ctx = lax.axis_index("ctx")
    exp = lax.axis_index("exp")
    row, core = lax.div(exp, 2), lax.rem(exp, 2)
    mate = row * 2 + (1 - core)
    cross = (1 - row) * 2 + core

    def remote(src, dst, kind, k, device):
        return pltpu.make_async_remote_copy(
            src_ref=src, dst_ref=dst, send_sem=send_sem.at[kind, k], recv_sem=recv_sem.at[kind, k],
            device_id=device, device_id_type=pl.DeviceIdType.MESH,
        )

    def partner(k):
        return exclusive_or(ctx, k, count)

    def direct(k):
        return remote(send_ref.at[partner(k)], rows.at[k, exp], 0, k, (partner(k), exp))

    def to_mate(k):
        return remote(rows.at[k, exp], rows.at[k, exp], 1, k, (ctx, mate))

    def to_cross(k):
        return remote(rows.at[k, exp], rows.at[k, exp], 2, k, (ctx, cross))

    def relay(k):
        return remote(rows.at[k, cross], rows.at[k, cross], 3, k, (ctx, mate))

    def part_to_mate(k):
        return remote(part.at[k, 1 - core], mate_in.at[k], 4, k, (ctx, mate))

    def sum_to_cross(k):
        return remote(mid.at[k], cross_in.at[k], 5, k, (ctx, cross))

    def give_back(k):
        return remote(done.at[k], out_ref.at[ctx], 6, k, (partner(k), exp))

    def self_in():
        return pltpu.make_async_copy(send_ref.at[ctx], rows.at[0, exp], local_sem.at[0])

    def self_out():
        return pltpu.make_async_copy(done.at[0], out_ref.at[ctx], local_sem.at[1])

    weights = [
        pltpu.make_async_copy(gate_hbm.at[0], both.at[:, pl.ds(0, units)], weight_sem.at[0]),
        pltpu.make_async_copy(up_hbm.at[0], both.at[:, pl.ds(units, units)], weight_sem.at[1]),
        pltpu.make_async_copy(down_hbm.at[0], down, weight_sem.at[2]),
    ]
    for copy in weights:
        copy.start()
    self_in().start()

    barrier = pltpu.get_barrier_semaphore()

    @pl.loop(1, count)
    def _(k):
        pl.semaphore_signal(
            barrier, inc=1, device_id=(partner(k), exp), device_id_type=pl.DeviceIdType.MESH
        )

    for other in (mate, cross):
        pl.semaphore_signal(
            barrier, inc=1, device_id=(ctx, other), device_id_type=pl.DeviceIdType.MESH
        )
    pl.semaphore_wait(barrier, count + 1)

    @pl.loop(1, count)
    def _(step):
        direct(ordered(step, count)).start()

    def compute(k):
        acc_both[...] = jnp.zeros_like(acc_both)
        acc_down[...] = jnp.zeros_like(acc_down)
        deep = DEEP

        @pl.loop(0, width // deep)
        def _(j):
            columns = pl.ds(pl.multiple_of(j * deep, deep), deep)
            acc_both[...] += jnp.dot(
                rows[k, :, pl.ds(0, tall), columns].reshape(4 * tall, deep),
                both[columns, :],
                preferred_element_type=F32,
            )
            acc_down[...] += lax.dot_general(
                rows[k, :, pl.ds(2 * capacity - tall, tall), columns].reshape(4 * tall, deep),
                down[:, columns],
                (((1,), (1,)), ((), ())),
                preferred_element_type=F32,
            )

        pre_gate = acc_both[:, :units].reshape(4, tall, units)[:, :capacity]
        pre_up = acc_both[:, units:].reshape(4, tall, units)[:, :capacity]
        raw_grad = acc_down[...].reshape(4, tall, units)[:, skip:]
        sig = jax.nn.sigmoid(pre_gate)
        act = pre_gate * sig
        slope = sig * (1.0 + pre_gate * (1.0 - sig))
        hidden = (act * pre_up).astype(BF16).astype(F32)
        dots = jnp.sum(hidden * raw_grad, axis=2, keepdims=True)
        high = dots.astype(BF16).astype(F32)
        tail = jnp.concatenate([high, dots - high], axis=1)
        tail = jnp.broadcast_to(tail, (4, 2 * capacity, LANES)).astype(BF16)
        for one in range(4):
            part[k, one % 2, one // 2, :, pl.ds(half, LANES)] = tail[one]
        grads[:, :units] = (raw_grad * pre_up * slope).reshape(4 * capacity, units).astype(BF16)
        grads[:, units:] = (raw_grad * act).reshape(4 * capacity, units).astype(BF16)

        @pl.loop(0, half // WIDE)
        def _(j):
            sides = []
            for side in range(2):
                start = pl.multiple_of(side * half + j * WIDE, WIDE)
                product = lax.dot_general(
                    grads[...],
                    both[pl.ds(start, WIDE), :],
                    (((1,), (1,)), ((), ())),
                    preferred_element_type=F32,
                )
                sides.append(product.reshape(4, capacity, WIDE))
            value = jnp.concatenate(sides, axis=1).astype(BF16)
            columns = pl.ds(pl.multiple_of(j * WIDE, WIDE), WIDE)
            for one in range(4):
                part[k, one % 2, one // 2, :, columns] = value[one]

    def stage(step, lag):
        return pl.when(jnp.logical_and(step >= lag, step < count + lag))

    @pl.loop(0, count + 4)
    def _(step):
        @pl.when(step == 0)
        def _():
            self_in().wait()

        @pl.when(jnp.logical_and(step >= 1, step < count))
        def _():
            direct(ordered(step, count)).wait_recv()

        @stage(step, 0)
        def _():
            k = ordered(step, count)
            to_cross(k).start()
            to_mate(k).start()

        @stage(step, 1)
        def _():
            k = ordered(step - 1, count)
            to_cross(k).wait_recv()
            relay(k).start()

        @pl.when(step == 2)
        def _():
            for copy in weights:
                copy.wait()

        @stage(step, 2)
        def _():
            k = ordered(step - 2, count)
            to_mate(k).wait_recv()
            relay(k).wait_recv()
            compute(k)
            part_to_mate(k).start()

        @stage(step, 3)
        def _():
            k = ordered(step - 3, count)
            part_to_mate(k).wait_recv()
            total = part[k, core, 1 - row].astype(F32) + mate_in[k, 1 - row].astype(F32)
            body, tail = carry(total, half, capacity)
            mid[k, :, pl.ds(0, half)] = body
            mid[k, :, pl.ds(half, LANES)] = tail
            sum_to_cross(k).start()

        def finish(k):
            sum_to_cross(k).wait_recv()
            total = part[k, core, row].astype(F32) + mate_in[k, row].astype(F32)
            total = total + cross_in[k].astype(F32)
            body, tail = carry(total, half, capacity)
            done[k, :, pl.ds(0, half)] = body
            done[k, :, pl.ds(half, LANES)] = tail

        @stage(step, 4)
        def _():
            finish(ordered(step - 4, count))

        @pl.when(step == 4)
        def _():
            self_out().start()

        @pl.when(jnp.logical_and(step > 4, step < count + 4))
        def _():
            give_back(ordered(step - 4, count)).start()

    self_out().wait()

    @pl.loop(1, count)
    def _(k):
        give_back(k).wait()
        direct(k).wait_send()

    @pl.loop(0, count)
    def _(k):
        to_mate(k).wait_send()
        to_cross(k).wait_send()
        relay(k).wait_send()
        part_to_mate(k).wait_send()
        sum_to_cross(k).wait_send()


def exchange_kernel(slots, capacity, w_gate, w_up, w_down):
    count, tall, width = slots.shape
    units = w_down.shape[1]
    wide = width // 2 + LANES
    rows_up = 4 * (-(-capacity // 16) * 16)
    vmem = pl.BlockSpec(memory_space=pltpu.VMEM)
    hbm = pl.BlockSpec(memory_space=pl.ANY)
    return pl.pallas_call(
        functools.partial(exchange_body, count, capacity),
        out_shape=jax.ShapeDtypeStruct((count, tall, wide), BF16),
        in_specs=[vmem, hbm, hbm, hbm],
        out_specs=vmem,
        scratch_shapes=[
            pltpu.VMEM((width, 2 * units), BF16),
            pltpu.VMEM((units, width), BF16),
            pltpu.VMEM((count, 4, tall, width), BF16),
            pltpu.VMEM((count, 2, 2, tall, wide), BF16),
            pltpu.VMEM((count, 2, tall, wide), BF16),
            pltpu.VMEM((count, tall, wide), BF16),
            pltpu.VMEM((count, tall, wide), BF16),
            pltpu.VMEM((count, tall, wide), BF16),
            pltpu.VMEM((rows_up, 2 * units), F32),
            pltpu.VMEM((rows_up, units), F32),
            pltpu.VMEM((4 * capacity, 2 * units), BF16),
            pltpu.SemaphoreType.DMA((3,)),
            pltpu.SemaphoreType.DMA((2,)),
            pltpu.SemaphoreType.DMA((7, count)),
            pltpu.SemaphoreType.DMA((7, count)),
        ],
        compiler_params=pltpu.CompilerParams(
            collective_id=0, has_side_effects=True, vmem_limit_bytes=56 * 2**20
        ),
    )(slots, w_gate, w_up, w_down)


def per_device(hidden_states, upstream, norm_gain, router, expert_ids, w_gate, w_up, w_down):
    tok_rows, model_width = hidden_states.shape
    experts = router.shape[1]
    capacity = 3 * tok_rows // (2 * experts)
    slot_total = experts * capacity
    labels = jnp.arange(experts, dtype=jnp.int32)
    chosen = (expert_ids[:, :, None] == labels).astype(F32)
    primary = chosen[:, 0, :]
    member = jnp.sum(chosen, axis=1)
    lower = (
        jnp.arange(tok_rows)[:, None] > jnp.arange(tok_rows)[None, :]
    ).astype(BF16)
    before = jnp.dot(lower, primary.astype(BF16), preferred_element_type=F32)
    slot_index = jnp.sum(before * primary, axis=1).astype(jnp.int32)
    target = expert_ids[:, 0] * capacity + slot_index

    widened = hidden_states.astype(F32)
    inverse = lax.rsqrt(jnp.mean(widened * widened, axis=1, keepdims=True) + EPSILON)
    normed = (widened * inverse * norm_gain).astype(BF16)

    use_kernel = capacity % 8 == 0 and lax.axis_size("exp") == 4 and experts == 8
    if use_kernel:
        place = expert_ids[:, 0] * (2 * capacity) + slot_index
        slots = pick(
            jnp.concatenate([place, place + capacity]),
            2 * slot_total,
            jnp.concatenate([normed, upstream], axis=0),
        )
        packed = exchange_kernel(
            slots.reshape(experts, 2 * capacity, model_width), capacity, w_gate, w_up, w_down
        )
        half = model_width // 2
        low, high = packed[:, :capacity], packed[:, capacity:]
        returned = jnp.concatenate([low[:, :, :half], high[:, :, :half]], axis=2)
        returned = returned.reshape(slot_total, model_width)
        dots = low[:, :, half].astype(F32) + high[:, :, half].astype(F32)
        dots = dots.reshape(slot_total)
    else:
        slots_up = pick(target, slot_total, upstream).reshape(experts, capacity, model_width)
        slots_normed = pick(target, slot_total, normed).reshape(experts, capacity, model_width)
        returned, dots = exchange_collective(
            slots_normed, slots_up, w_gate[0], w_up[0], w_down[0]
        )

    logits = jnp.dot(normed, router, preferred_element_type=F32)
    probability = jax.nn.softmax(logits, axis=1)
    top_prob = jnp.sum(probability * primary, axis=1)
    route_mass = jnp.sum(probability * member, axis=1)
    gate_value = top_prob / route_mass

    own = target[:, None] == jnp.arange(slot_total, dtype=jnp.int32)[None, :]
    raw_back = jnp.dot(own.astype(BF16), returned, preferred_element_type=F32)
    gate_grad = jnp.sum(jnp.where(own, dots[None, :], 0.0), axis=1)
    expert_grad = gate_value[:, None] * raw_back
    prob_grad = gate_grad[:, None] * (
        primary / route_mass[:, None] - (top_prob / (route_mass * route_mass))[:, None] * member
    )
    logit_grad = probability * (prob_grad - jnp.sum(probability * prob_grad, axis=1, keepdims=True))
    normed_grad = expert_grad + jnp.dot(
        logit_grad, router.astype(F32).T, precision=lax.Precision.HIGHEST
    )
    scaled = normed_grad * norm_gain
    grad_input = (
        inverse * scaled
        - widened * inverse**3 * jnp.sum(scaled * widened, axis=1, keepdims=True) / model_width
    )
    return grad_input.astype(BF16)


def solution(mesh):
    placed = (
        P(("ctx", "exp"), None),
        P(("ctx", "exp"), None),
        P(),
        P(),
        P(("ctx", "exp"), None),
        P("ctx", None, "exp"),
        P("ctx", None, "exp"),
        P("ctx", "exp", None),
    )
    return jax.shard_map(
        per_device, mesh=mesh, in_specs=placed, out_specs=P(("ctx", "exp"), None), check_vma=False
    )
```

```python
import functools

import jax
import jax.numpy as jnp
from jax import lax
from jax.experimental import pallas as pl
from jax.experimental.pallas import tpu as pltpu
from jax.sharding import PartitionSpec as P

EPSILON = 1e-06
F32 = jnp.float32
BF16 = jnp.bfloat16
LANES = 128
DEEP = 1024
WIDE = 512


def pick(rows_of, total, values):
    hot = (rows_of[None, :] == jnp.arange(total, dtype=jnp.int32)[:, None]).astype(BF16)
    return jnp.dot(hot, values, preferred_element_type=F32).astype(BF16)


def expert_math(normed_rows, up_rows, gate_block, up_block, down_block):
    pre_gate = jnp.dot(normed_rows, gate_block, preferred_element_type=F32)
    pre_up = jnp.dot(normed_rows, up_block, preferred_element_type=F32)
    raw_grad = lax.dot_general(
        up_rows, down_block, (((1,), (1,)), ((), ())), preferred_element_type=F32
    )
    sig = jax.nn.sigmoid(pre_gate)
    act = pre_gate * sig
    slope = sig * (1.0 + pre_gate * (1.0 - sig))
    hidden = (act * pre_up).astype(BF16).astype(F32)
    dots = jnp.sum(hidden * raw_grad, axis=1)
    grad_gate = (raw_grad * pre_up * slope).astype(BF16)
    grad_up = (raw_grad * act).astype(BF16)
    back = lax.dot_general(
        grad_gate, gate_block, (((1,), (1,)), ((), ())), preferred_element_type=F32
    ) + lax.dot_general(grad_up, up_block, (((1,), (1,)), ((), ())), preferred_element_type=F32)
    return back, dots


def exchange_collective(slots_normed, slots_up, gate_block, up_block, down_block):
    experts, capacity, width = slots_normed.shape

    def dispatch(shaped):
        moved = lax.all_to_all(shaped, "ctx", split_axis=0, concat_axis=0, tiled=True)
        return lax.all_gather(
            moved.reshape(experts * capacity, width), "exp", axis=0, tiled=True
        )

    back, dots = expert_math(
        dispatch(slots_normed), dispatch(slots_up), gate_block, up_block, down_block
    )
    summed = lax.psum_scatter(back.astype(BF16), "exp", scatter_dimension=0, tiled=True)
    dot_sum = lax.psum_scatter(dots, "exp", scatter_dimension=0, tiled=True)
    returned = lax.all_to_all(
        summed.reshape(experts, capacity, width), "ctx", split_axis=0, concat_axis=0, tiled=True
    )
    dot_back = lax.all_to_all(
        dot_sum.reshape(experts, capacity), "ctx", split_axis=0, concat_axis=0, tiled=True
    )
    return returned.reshape(experts * capacity, width), dot_back.reshape(experts * capacity)


def exclusive_or(left, right, count):
    total, bit = 0, 1
    while bit < count:
        total = total + bit * lax.rem(lax.div(left, bit) + lax.div(right, bit), 2)
        bit *= 2
    return total


def ordered(step, count):
    far = lax.div(step + 5, count)
    late = lax.div(step + 1, count)
    return step + far - 5 * late


def carry(total, width, capacity):
    dots = total[:capacity, width:] + total[capacity:, width:]
    high = dots.astype(BF16).astype(F32)
    return total[:, :width].astype(BF16), jnp.concatenate([high, dots - high], axis=0).astype(BF16)


def exchange_body(
    count, capacity, send_ref, gate_hbm, up_hbm, down_hbm, out_ref,
    both, down, rows, part, mate_in, mid, cross_in, done, acc_both, acc_down, grads,
    weight_sem, local_sem, send_sem, recv_sem,
):
    width = send_ref.shape[2]
    half = width // 2
    units = down.shape[0]
    tall = -(-capacity // 16) * 16
    skip = tall - capacity
    ctx = lax.axis_index("ctx")
    exp = lax.axis_index("exp")
    row, core = lax.div(exp, 2), lax.rem(exp, 2)
    mate = row * 2 + (1 - core)
    cross = (1 - row) * 2 + core

    def remote(src, dst, kind, k, device):
        return pltpu.make_async_remote_copy(
            src_ref=src, dst_ref=dst, send_sem=send_sem.at[kind, k], recv_sem=recv_sem.at[kind, k],
            device_id=device, device_id_type=pl.DeviceIdType.MESH,
        )

    def partner(k):
        return exclusive_or(ctx, k, count)

    def direct(k):
        return remote(send_ref.at[partner(k)], rows.at[k, exp], 0, k, (partner(k), exp))

    def to_mate(k):
        return remote(rows.at[k, exp], rows.at[k, exp], 1, k, (ctx, mate))

    def to_cross(k):
        return remote(rows.at[k, exp], rows.at[k, exp], 2, k, (ctx, cross))

    def relay(k):
        return remote(rows.at[k, cross], rows.at[k, cross], 3, k, (ctx, mate))

    def part_to_mate(k):
        return remote(part.at[k, 1 - core], mate_in.at[k], 4, k, (ctx, mate))

    def sum_to_cross(k):
        return remote(mid.at[k], cross_in.at[k], 5, k, (ctx, cross))

    def give_back(k):
        return remote(done.at[k], out_ref.at[ctx], 6, k, (partner(k), exp))

    def self_in():
        return pltpu.make_async_copy(send_ref.at[ctx], rows.at[0, exp], local_sem.at[0])

    def self_out():
        return pltpu.make_async_copy(done.at[0], out_ref.at[ctx], local_sem.at[1])

    weights = [
        pltpu.make_async_copy(gate_hbm.at[0], both.at[:, pl.ds(0, units)], weight_sem.at[0]),
        pltpu.make_async_copy(up_hbm.at[0], both.at[:, pl.ds(units, units)], weight_sem.at[1]),
        pltpu.make_async_copy(down_hbm.at[0], down, weight_sem.at[2]),
    ]
    for copy in weights:
        copy.start()
    self_in().start()

    barrier = pltpu.get_barrier_semaphore()

    @pl.loop(1, count)
    def _(k):
        pl.semaphore_signal(
            barrier, inc=1, device_id=(partner(k), exp), device_id_type=pl.DeviceIdType.MESH
        )

    for other in (mate, cross):
        pl.semaphore_signal(
            barrier, inc=1, device_id=(ctx, other), device_id_type=pl.DeviceIdType.MESH
        )
    pl.semaphore_wait(barrier, count + 1)

    for k in (1, 4, 2):
        direct(k).start()

    def compute(k):
        acc_both[...] = jnp.zeros_like(acc_both)
        acc_down[...] = jnp.zeros_like(acc_down)
        deep = DEEP

        @pl.loop(0, width // deep)
        def _(j):
            columns = pl.ds(pl.multiple_of(j * deep, deep), deep)
            acc_both[...] += jnp.dot(
                rows[k, :, pl.ds(0, tall), columns].reshape(4 * tall, deep),
                both[columns, :],
                preferred_element_type=F32,
            )
            acc_down[...] += lax.dot_general(
                rows[k, :, pl.ds(2 * capacity - tall, tall), columns].reshape(4 * tall, deep),
                down[:, columns],
                (((1,), (1,)), ((), ())),
                preferred_element_type=F32,
            )

        pre_gate = acc_both[:, :units].reshape(4, tall, units)[:, :capacity]
        pre_up = acc_both[:, units:].reshape(4, tall, units)[:, :capacity]
        raw_grad = acc_down[...].reshape(4, tall, units)[:, skip:]
        sig = jax.nn.sigmoid(pre_gate)
        act = pre_gate * sig
        slope = sig * (1.0 + pre_gate * (1.0 - sig))
        hidden = (act * pre_up).astype(BF16).astype(F32)
        dots = jnp.sum(hidden * raw_grad, axis=2, keepdims=True)
        high = dots.astype(BF16).astype(F32)
        tail = jnp.concatenate([high, dots - high], axis=1)
        tail = jnp.broadcast_to(tail, (4, 2 * capacity, LANES)).astype(BF16)
        for one in range(4):
            part[k, one % 2, one // 2, :, pl.ds(half, LANES)] = tail[one]
        grads[:, :units] = (raw_grad * pre_up * slope).reshape(4 * capacity, units).astype(BF16)
        grads[:, units:] = (raw_grad * act).reshape(4 * capacity, units).astype(BF16)

        @pl.loop(0, half // WIDE)
        def _(j):
            sides = []
            for side in range(2):
                start = pl.multiple_of(side * half + j * WIDE, WIDE)
                product = lax.dot_general(
                    grads[...],
                    both[pl.ds(start, WIDE), :],
                    (((1,), (1,)), ((), ())),
                    preferred_element_type=F32,
                )
                sides.append(product.reshape(4, capacity, WIDE))
            value = jnp.concatenate(sides, axis=1).astype(BF16)
            columns = pl.ds(pl.multiple_of(j * WIDE, WIDE), WIDE)
            for one in range(4):
                part[k, one % 2, one // 2, :, columns] = value[one]

    def stage(step, lag):
        return pl.when(jnp.logical_and(step >= lag, step < count + lag))

    @pl.loop(0, count + 4)
    def _(step):
        @pl.when(step == 0)
        def _():
            self_in().wait()

        @pl.when(jnp.logical_and(step >= 1, step < count))
        def _():
            direct(ordered(step, count)).wait_recv()

        @pl.when(step == 2)
        def _():
            direct(5).start()

        @pl.when(step == 4)
        def _():
            direct(6).start()

        @pl.when(step == 5)
        def _():
            direct(7).start()
            direct(3).start()

        @stage(step, 0)
        def _():
            k = ordered(step, count)
            to_cross(k).start()
            to_mate(k).start()

        @stage(step, 1)
        def _():
            k = ordered(step - 1, count)
            to_cross(k).wait_recv()
            relay(k).start()

        @pl.when(step == 2)
        def _():
            for copy in weights:
                copy.wait()

        @stage(step, 2)
        def _():
            k = ordered(step - 2, count)
            to_mate(k).wait_recv()
            relay(k).wait_recv()
            compute(k)
            part_to_mate(k).start()

        @stage(step, 3)
        def _():
            k = ordered(step - 3, count)
            part_to_mate(k).wait_recv()
            total = part[k, core, 1 - row].astype(F32) + mate_in[k, 1 - row].astype(F32)
            body, tail = carry(total, half, capacity)
            mid[k, :, pl.ds(0, half)] = body
            mid[k, :, pl.ds(half, LANES)] = tail
            sum_to_cross(k).start()

        def finish(k):
            sum_to_cross(k).wait_recv()
            total = part[k, core, row].astype(F32) + mate_in[k, row].astype(F32)
            total = total + cross_in[k].astype(F32)
            body, tail = carry(total, half, capacity)
            done[k, :, pl.ds(0, half)] = body
            done[k, :, pl.ds(half, LANES)] = tail

        @stage(step, 4)
        def _():
            finish(ordered(step - 4, count))

        @pl.when(step == 4)
        def _():
            self_out().start()

        @pl.when(jnp.logical_and(step > 4, step < count + 4))
        def _():
            give_back(ordered(step - 4, count)).start()

    self_out().wait()

    @pl.loop(1, count)
    def _(k):
        give_back(k).wait()
        direct(k).wait_send()

    @pl.loop(0, count)
    def _(k):
        to_mate(k).wait_send()
        to_cross(k).wait_send()
        relay(k).wait_send()
        part_to_mate(k).wait_send()
        sum_to_cross(k).wait_send()


def exchange_kernel(slots, capacity, w_gate, w_up, w_down):
    count, tall, width = slots.shape
    units = w_down.shape[1]
    wide = width // 2 + LANES
    rows_up = 4 * (-(-capacity // 16) * 16)
    vmem = pl.BlockSpec(memory_space=pltpu.VMEM)
    hbm = pl.BlockSpec(memory_space=pl.ANY)
    return pl.pallas_call(
        functools.partial(exchange_body, count, capacity),
        out_shape=jax.ShapeDtypeStruct((count, tall, wide), BF16),
        in_specs=[vmem, hbm, hbm, hbm],
        out_specs=vmem,
        scratch_shapes=[
            pltpu.VMEM((width, 2 * units), BF16),
            pltpu.VMEM((units, width), BF16),
            pltpu.VMEM((count, 4, tall, width), BF16),
            pltpu.VMEM((count, 2, 2, tall, wide), BF16),
            pltpu.VMEM((count, 2, tall, wide), BF16),
            pltpu.VMEM((count, tall, wide), BF16),
            pltpu.VMEM((count, tall, wide), BF16),
            pltpu.VMEM((count, tall, wide), BF16),
            pltpu.VMEM((rows_up, 2 * units), F32),
            pltpu.VMEM((rows_up, units), F32),
            pltpu.VMEM((4 * capacity, 2 * units), BF16),
            pltpu.SemaphoreType.DMA((3,)),
            pltpu.SemaphoreType.DMA((2,)),
            pltpu.SemaphoreType.DMA((7, count)),
            pltpu.SemaphoreType.DMA((7, count)),
        ],
        compiler_params=pltpu.CompilerParams(
            collective_id=0, has_side_effects=True, vmem_limit_bytes=56 * 2**20
        ),
    )(slots, w_gate, w_up, w_down)


def per_device(hidden_states, upstream, norm_gain, router, expert_ids, w_gate, w_up, w_down):
    tok_rows, model_width = hidden_states.shape
    experts = router.shape[1]
    capacity = 3 * tok_rows // (2 * experts)
    slot_total = experts * capacity
    labels = jnp.arange(experts, dtype=jnp.int32)
    chosen = (expert_ids[:, :, None] == labels).astype(F32)
    primary = chosen[:, 0, :]
    member = jnp.sum(chosen, axis=1)
    lower = (
        jnp.arange(tok_rows)[:, None] > jnp.arange(tok_rows)[None, :]
    ).astype(BF16)
    before = jnp.dot(lower, primary.astype(BF16), preferred_element_type=F32)
    slot_index = jnp.sum(before * primary, axis=1).astype(jnp.int32)
    target = expert_ids[:, 0] * capacity + slot_index

    widened = hidden_states.astype(F32)
    inverse = lax.rsqrt(jnp.mean(widened * widened, axis=1, keepdims=True) + EPSILON)
    normed = (widened * inverse * norm_gain).astype(BF16)

    use_kernel = capacity % 8 == 0 and lax.axis_size("exp") == 4 and experts == 8
    if use_kernel:
        place = expert_ids[:, 0] * (2 * capacity) + slot_index
        slots = pick(
            jnp.concatenate([place, place + capacity]),
            2 * slot_total,
            jnp.concatenate([normed, upstream], axis=0),
        )
        packed = exchange_kernel(
            slots.reshape(experts, 2 * capacity, model_width), capacity, w_gate, w_up, w_down
        )
        half = model_width // 2
        own = (place[:, None] == jnp.arange(2 * slot_total, dtype=jnp.int32)[None, :]).astype(BF16)
        own_high = (
            place[:, None] + capacity == jnp.arange(2 * slot_total, dtype=jnp.int32)[None, :]
        ).astype(BF16)
        packed = packed.reshape(2 * slot_total, half + LANES)
        low = jnp.dot(own, packed, preferred_element_type=F32)
        high = jnp.dot(own_high, packed, preferred_element_type=F32)
        raw_back = jnp.concatenate([low[:, :half], high[:, :half]], axis=1)
        gate_grad = low[:, half] + high[:, half]
    else:
        slots_up = pick(target, slot_total, upstream).reshape(experts, capacity, model_width)
        slots_normed = pick(target, slot_total, normed).reshape(experts, capacity, model_width)
        returned, dots = exchange_collective(
            slots_normed, slots_up, w_gate[0], w_up[0], w_down[0]
        )
        own = target[:, None] == jnp.arange(slot_total, dtype=jnp.int32)[None, :]
        raw_back = jnp.dot(own.astype(BF16), returned, preferred_element_type=F32)
        gate_grad = jnp.sum(jnp.where(own, dots[None, :], 0.0), axis=1)

    logits = jnp.dot(normed, router, preferred_element_type=F32)
    probability = jax.nn.softmax(logits, axis=1)
    top_prob = jnp.sum(probability * primary, axis=1)
    route_mass = jnp.sum(probability * member, axis=1)
    gate_value = top_prob / route_mass

    expert_grad = gate_value[:, None] * raw_back
    prob_grad = gate_grad[:, None] * (
        primary / route_mass[:, None] - (top_prob / (route_mass * route_mass))[:, None] * member
    )
    logit_grad = probability * (prob_grad - jnp.sum(probability * prob_grad, axis=1, keepdims=True))
    normed_grad = expert_grad + jnp.dot(
        logit_grad, router.astype(F32).T, precision=lax.Precision.HIGHEST
    )
    scaled = normed_grad * norm_gain
    grad_input = (
        inverse * scaled
        - widened * inverse**3 * jnp.sum(scaled * widened, axis=1, keepdims=True) / model_width
    )
    return grad_input.astype(BF16)


def solution(mesh):
    placed = (
        P(("ctx", "exp"), None),
        P(("ctx", "exp"), None),
        P(),
        P(),
        P(("ctx", "exp"), None),
        P("ctx", None, "exp"),
        P("ctx", None, "exp"),
        P("ctx", "exp", None),
    )
    return jax.shard_map(
        per_device, mesh=mesh, in_specs=placed, out_specs=P(("ctx", "exp"), None), check_vma=False
    )
```
